32 devices in a mesh: gx: 4 (over z), gy: 8 (over y, x, core).
Axes of the slice: x: 2, y: 2, z: 4, core: 2. Of those that a mesh axis runs over, the one named last changes fastest.
Arguments:
- tokens: bfloat16 [4096, 2048], P('gy', 'gx'), may hold values from -6 to 6
- gain_attn: float32 [2048], P('gx'), may hold values from 0.25 to 1.75
- w_qkv: bfloat16 [2048, 3, 2048], P('gx', None, 'gy'), may hold values from -0.125 to 0.125
- w_out: bfloat16 [2048, 2048], P('gy', 'gx'), may hold values from -0.5 to 0.5
- gain_mlp: float32 [2048], P('gx'), may hold values from 0.25 to 1.75
- w_gate_up: bfloat16 [2048, 2, 8192], P('gx', None, 'gy'), may hold values from -0.125 to 0.125
- w_down: bfloat16 [8192, 2048], P('gy', 'gx'), may hold values from -0.0625 to 0.0625
- segments: int32 [4, 1024], P('gx'), may hold values from 0 to 1, never falling along the last dimension, each value on 1 to 768 neighbouring positions
- grad_output: bfloat16 [4096, 2048], P('gy', 'gx'), may hold values from -6 to 6
Outputs:
- output: bfloat16 [4096, 2048], P('gy', 'gx')
- grad_tokens: float32 [4096, 2048], P('gy', 'gx')
- grad_gain_attn: float32 [2048], P('gx')
- grad_qkv: float32 [2048, 3, 2048], P('gx', None, 'gy')
- grad_out: float32 [2048, 2048], P('gy', 'gx')
- grad_gain_mlp: float32 [2048], P('gx')
- grad_gate_up: float32 [2048, 2, 8192], P('gx', None, 'gy')
- grad_down: float32 [8192, 2048], P('gy', 'gx')
The draws below stay inside these ranges and needn't reach their ends.
All inputs are finite; a program needn't handle non-finite values.
Results may differ from the reference program's by a relative error of at most 0.02.
Values may be sent and summed in bfloat16 or wider, within the bound.
No kernel may reach another device: no remote copies, remote signals or barrier semaphores. Data moves between devices by JAX's collectives and lax.ppermute only.
A program may use at most 320 MiB of HBM per device.

```python
import math
import jax
import jax.numpy as jnp
import numpy as np
from jax import lax

D = 2048
H = 32
HD = 64
FF = 8192
TOKENS = 4096
L = 1024
NSEQ = 4


def levels(rng, extent, pieces, smallest, high):
    level = 1.0
    for axis_at, parts in pieces:
        steps = jax.random.uniform(jax.random.fold_in(jax.random.fold_in(rng, 6), axis_at), (parts,), jnp.float32, smallest / len(pieces), high / len(pieces))
        level = level * jnp.repeat(jnp.exp(steps), extent[axis_at] // parts).reshape((-1,) + (1,) * (len(extent) - 1 - axis_at))
    return level


def profile(number_of, total, most, lean):
    portions = [(1 << 20) // math.isqrt(rank ** lean) + 1 for rank in range(2, number_of + 1)]
    surplus, holding = total - most - (number_of - 1), [1] * (number_of - 1)
    while surplus > 0:
        candidates = [i for i in range(number_of - 1) if holding[i] < most]
        pool, left = sum([portions[i] for i in candidates]), surplus
        for i in candidates:
            more = min(most - holding[i], max(1, left * portions[i] // pool), surplus)
            holding[i] = holding[i] + more
            surplus = surplus - more
    return np.array([most] + holding)


def uneven_parts(key, number_of, total, limit, skew):
    if number_of == 2:
        one = jax.random.randint(key, (), max(1, total - limit), min(limit, total - 1) + 1)
        return jnp.stack([one, total - one])
    sizes = jnp.asarray(profile(number_of, total, limit, skew), jnp.int32)
    couples = (number_of - 1) // 2
    source_of, receiver = sizes[1:1 + 2 * couples:2], sizes[2:2 + 2 * couples:2]
    slack = jnp.minimum(source_of - 1, limit - receiver)
    passed = jax.random.randint(jax.random.fold_in(key, 1), (couples,), 0, 1 << 20) % (slack + 1)
    sizes = sizes.at[1:1 + 2 * couples:2].set(source_of - passed).at[2:2 + 2 * couples:2].set(receiver + passed)
    return sizes[jax.random.permutation(jax.random.fold_in(key, 2), number_of)]


def noise(rng, dims, width, most, cuts=(), kind=jnp.bfloat16):
    values = jax.random.normal(rng, dims, jnp.float32) * width
    if len(cuts) > 0:
        values = levels(rng, dims, cuts, -0.22, 0.18) * values
    return jnp.clip(values, min=-most, max=most).astype(kind)


def setup_inputs(seed: int = 0) -> dict:
    key_of = jax.random.split(jax.random.key(seed), 10)
    tokens = noise(key_of[0], (TOKENS, D), 1.0, 6.0, ((0, 8), (1, 4)))
    gain_attn = jnp.clip(1.0 + 0.15 * jax.random.normal(key_of[1], (D,), jnp.float32), 0.25, 1.75)
    w_qkv = noise(key_of[2], (D, 3, D), D ** -0.5, 0.125, ((0, 4), (2, 8)))
    w_out = noise(key_of[3], (D, D), (D // 16) ** -0.5, 0.5, ((0, 8), (1, 4)))
    gain_mlp = jnp.clip(1.0 + 0.15 * jax.random.normal(key_of[4], (D,), jnp.float32), 0.25, 1.75)
    w_gate_up = noise(key_of[5], (D, 2, FF), D ** -0.5, 0.125, ((0, 4), (2, 8)))
    w_down = noise(key_of[6], (FF, D), FF ** -0.5, 0.0625, ((0, 8), (1, 4)))
    segments = jax.vmap(lambda own: jnp.searchsorted(jnp.cumsum(uneven_parts(own, max(2, L // 512), L, L * 3 // 4, 2)), jnp.arange(L), side="right"))(jax.random.split(key_of[7], NSEQ)).reshape((NSEQ, L)).astype(jnp.int32)
    grad_output = noise(key_of[8], (TOKENS, D), 1.0, 6.0, ((0, 8), (1, 4)))
    return {"tokens": tokens, "gain_attn": gain_attn, "w_qkv": w_qkv, "w_out": w_out, "gain_mlp": gain_mlp, "w_gate_up": w_gate_up, "w_down": w_down, "segments": segments, "grad_output": grad_output}


EPS = 1e-05
THETA = 130000.0
NEG = -1e+30

@jax.custom_vjp
def low(v):
    return lax.optimization_barrier(v.astype(jnp.bfloat16)).astype(jnp.float32)

@jax.custom_vjp
def low_back(v):
    return v

def low_keep(v):
    return (low(v), None)

def low_pass(kept, grad):
    return (grad,)

def back_keep(v):
    return (v, None)

def back_low(kept, grad):
    return (low(grad),)
low.defvjp(low_keep, low_pass)
low_back.defvjp(back_keep, back_low)

def doc_positions(segs):
    index = jnp.broadcast_to(jnp.arange(segs.shape[1], dtype=jnp.int32)[None, :], segs.shape)
    before = jnp.concatenate([segs[:, :1] - 1, segs[:, :-1]], axis=1)
    starts = jnp.where(segs != before, index, jnp.zeros_like(index))
    return index - lax.cummax(starts, axis=1)

def turn(value):
    half = value.shape[-1] // 2
    return jnp.concatenate([-value[..., half:], value[..., :half]], axis=-1)

def rotate(value, positions):
    half = HD // 2
    freq = THETA ** (-jnp.arange(half, dtype=jnp.float32) * 2.0 / HD)
    angle = positions.astype(jnp.float32)[:, None] * freq[None, :]
    angle = jnp.concatenate([angle, angle], axis=1)[:, None, :]
    return value * jnp.cos(angle) + turn(value) * jnp.sin(angle)

def normalize(value, gain):
    scale = lax.rsqrt(lax.optimization_barrier(jnp.mean(value * value, axis=1, keepdims=True)) + EPS)
    return value * scale * gain[None, :]

def allowed(seg, start, block):
    qidx = start + jnp.arange(block, dtype=jnp.int32)
    kidx = jnp.arange(seg.shape[0], dtype=jnp.int32)
    qseg = lax.dynamic_slice_in_dim(seg, start, block, 0)
    return (qseg[:, None] == seg[None, :]) & (kidx[None, :] <= qidx[:, None])

def attend_sequence(args):
    query, key, value, seg = args
    block = min(512, L)
    scale = 1.0 / HD ** 0.5

    def piece(start):
        qblock = lax.dynamic_slice_in_dim(query, start, block, 0)
        raw = low_back(jnp.einsum('qhd,khd->hqk', qblock, key, precision=lax.Precision.HIGHEST))
        scores = jnp.where(allowed(seg, start, block)[None], raw * scale, NEG)
        probs = jax.nn.softmax(scores, axis=2)
        return jnp.einsum('hqk,khd->qhd', low(probs), value, precision=lax.Precision.HIGHEST)
    starts = jnp.arange(L // block, dtype=jnp.int32) * block
    out = lax.map(jax.checkpoint(piece), starts)
    return out.reshape(query.shape)

def forward(x, gain_attn, w_qkv, w_out, gain_mlp, w_gate_up, w_down, segments):
    hp = lax.Precision.HIGHEST
    positions = doc_positions(segments).reshape(-1)
    normed_a = low(normalize(x, gain_attn))
    pre = low_back(jnp.einsum('td,dce->tce', normed_a, w_qkv, precision=hp))
    pre = pre.reshape(TOKENS, 3, H, HD)
    query = low(rotate(pre[:, 0], positions)).reshape(NSEQ, L, H, HD)
    key = low(rotate(pre[:, 1], positions)).reshape(NSEQ, L, H, HD)
    value = low(pre[:, 2]).reshape(NSEQ, L, H, HD)
    att = lax.map(jax.checkpoint(attend_sequence), (query, key, value, segments))
    att = low_back(low(att.reshape(TOKENS, D)))
    attn_out = low_back(jnp.dot(att, w_out, precision=hp))
    mid = x + attn_out
    normed_m = low(normalize(mid, gain_mlp))
    gate_up = low_back(jnp.einsum('td,dcf->tcf', normed_m, w_gate_up, precision=hp))
    hidden = low(jax.nn.silu(gate_up[:, 0]) * gate_up[:, 1])
    mlp_out = low_back(jnp.dot(hidden, w_down, precision=hp))
    return mid + mlp_out

def reference(tokens, gain_attn, w_qkv, w_out, gain_mlp, w_gate_up, w_down, segments, grad_output):
    f32 = jnp.float32

    def closed(x, ga, wq, wo, gm, wg, wd):
        return forward(x, ga, wq, wo, gm, wg, wd, segments)
    result, pullback = jax.vjp(closed, tokens.astype(f32), gain_attn.astype(f32), w_qkv.astype(f32), w_out.astype(f32), gain_mlp.astype(f32), w_gate_up.astype(f32), w_down.astype(f32))
    grads = pullback(grad_output.astype(f32))
    return (result.astype(jnp.bfloat16), grads[0], grads[1], grads[2], grads[3], grads[4], grads[5], grads[6])
```

```python
import functools

import jax
import jax.numpy as jnp
from jax import lax
from jax.experimental import pallas as pl
from jax.experimental.pallas import tpu as pltpu
from jax.sharding import PartitionSpec as P

HD = 64
EPS = 1e-05
THETA = 130000.0
NEG = -1e30
BF16 = jnp.bfloat16
F32 = jnp.float32


def dot(left, right, dims):
    return lax.dot_general(left, right, (dims, ((), ())), preferred_element_type=F32)


def to_rows(block):
    gx, gy = lax.axis_size("gx"), lax.axis_size("gy")
    g = gy // gx
    i, j = lax.axis_index("gx"), lax.axis_index("gy")
    parts = block.reshape(gx, block.shape[0] // gx, block.shape[1])
    came = []
    for k in range(gx):
        perm = [
            (a * gy + s * g + r, s * gy + r * gx + (a + k) % gx)
            for a in range(gx)
            for s in range(gx)
            for r in range(g)
        ]
        part = lax.dynamic_index_in_dim(parts, (i + k) % gx, 0, keepdims=False)
        came.append(lax.ppermute(part, ("gx", "gy"), perm))
    q = j % gx
    return jnp.concatenate([lax.select_n((q - a) % gx, *came) for a in range(gx)], axis=1)


def to_blocks(rows):
    gx, gy = lax.axis_size("gx"), lax.axis_size("gy")
    g = gy // gx
    i, j = lax.axis_index("gx"), lax.axis_index("gy")
    q = j % gx
    width = rows.shape[1] // gx
    parts = [rows[:, a * width : (a + 1) * width] for a in range(gx)]
    came = []
    for k in range(gx):
        perm = [
            (s * gy + r * gx + (a + k) % gx, a * gy + s * g + r)
            for a in range(gx)
            for s in range(gx)
            for r in range(g)
        ]
        came.append(lax.ppermute(lax.select_n((q - k) % gx, *parts), ("gx", "gy"), perm))
    return jnp.concatenate([lax.select_n((b - i) % gx, *came) for b in range(gx)], axis=0)


def swap(value, bit):
    size = lax.axis_size("gy")
    return lax.ppermute(value, "gy", [(a, a ^ bit) for a in range(size)])


def mine(bit):
    return (lax.axis_index("gy") & bit) != 0


def joined(value, bit, axis):
    other = swap(value, bit)
    up = mine(bit)
    return jnp.stack([jnp.where(up, other, value), jnp.where(up, value, other)], axis=axis)


def gather_rows(rows):
    if lax.axis_size("gy") != 8:
        return lax.all_gather(rows, "gy", axis=0, tiled=True)
    n, width = rows.shape
    half = width // 2
    left, right = rows[:, :half], rows[:, half:]
    left = joined(joined(left, 2, 0), 4, 0)
    right = joined(joined(right, 4, 0), 2, 1)
    both = [joined(v.reshape(4, n, half), 1, 1).reshape(8 * n, half) for v in (left, right)]
    return jnp.concatenate(both, axis=1)


def halves(value, bit, axis):
    up = mine(bit)
    low, high = lax.index_in_dim(value, 0, axis, False), lax.index_in_dim(value, 1, axis, False)
    return jnp.where(up, high, low), jnp.where(up, low, high)


def reduced(value, bit, axis):
    keep, send = halves(value, bit, axis)
    return keep.astype(F32) + swap(send.astype(BF16), bit).astype(F32)


def project_sum(left, weight, dims):
    if lax.axis_size("gy") != 8:
        part = dot(left, weight, dims).astype(BF16)
        return lax.psum_scatter(part, "gy", scatter_dimension=0, tiled=True).astype(F32)
    n = left.shape[0] // 8
    keep, send = halves(left.reshape(4, 2, n, left.shape[1]), 1, 1)
    other = swap(dot(send.reshape(4 * n, -1), weight, dims).astype(BF16), 1)
    total = dot(keep.reshape(4 * n, -1), weight, dims) + other.astype(F32)
    total = total.reshape(2, 2, n, -1)
    half = total.shape[3] // 2
    left_half = reduced(reduced(total[..., :half], 4, 0), 2, 0)
    right_half = reduced(reduced(total[..., half:], 2, 1), 4, 0)
    return jnp.concatenate([left_half, right_half], axis=1)


def normalize(value, gain):
    scale = lax.rsqrt(jnp.mean(value * value, axis=1, keepdims=True) + EPS)
    return (value * scale * gain[None, :]).astype(BF16), scale


def normalize_back(value, gain, scale, grad):
    weighted = grad * gain[None, :]
    inner = jnp.mean(weighted * value, axis=1, keepdims=True)
    grad_gain = jnp.sum(grad * value * scale, axis=0)
    return scale * weighted - value * (scale * scale * scale * inner), grad_gain


def doc_starts(segs):
    index = jnp.broadcast_to(jnp.arange(segs.shape[1], dtype=jnp.int32)[None, :], segs.shape)
    before = jnp.concatenate([segs[:, :1] - 1, segs[:, :-1]], axis=1)
    return lax.cummax(jnp.where(segs != before, index, jnp.zeros_like(index)), axis=1)


def rotary(positions, width):
    half = HD // 2
    freq = THETA ** (-jnp.arange(half, dtype=F32) * 2.0 / HD)
    angle = positions.astype(F32)[:, None] * freq[None, :]
    copies = width // half
    return jnp.tile(jnp.cos(angle), (1, copies)), jnp.tile(jnp.sin(angle), (1, copies))


def turn(value):
    width = value.shape[1]
    half = HD // 2
    pieces = []
    for at in range(0, width, HD):
        pieces += [-value[:, at + half : at + HD], value[:, at : at + half]]
    return jnp.concatenate(pieces, axis=1)


def masked_scores(query, key, start, first):
    scores = dot(query, key, ((1,), (1,)))
    kidx = lax.broadcasted_iota(jnp.int32, scores.shape, 1)
    qidx = lax.broadcasted_iota(jnp.int32, scores.shape, 0) + first
    return jnp.where((kidx >= start) & (kidx <= qidx), scores, NEG)


def forward_kernel(block, q_ref, k_ref, v_ref, cos_ref, sin_ref, start_ref, att, qo, ko, vo, lse):
    cosine, sine = cos_ref[...], sin_ref[...]
    q, k = q_ref[...], k_ref[...]
    qo[...] = (q * cosine + turn(q) * sine).astype(BF16)
    ko[...] = (k * cosine + turn(k) * sine).astype(BF16)
    vo[...] = v_ref[...].astype(BF16)
    length, width = q.shape
    for at in range(0, width, HD):
        lanes = slice(at, at + HD)
        for first in range(0, length, block):
            rows, high = slice(first, first + block), first + block
            query = qo[rows, lanes] * BF16(HD**-0.5)
            scores = masked_scores(query, ko[:high, lanes], start_ref[rows, :], first)
            peak = jnp.max(scores, axis=1, keepdims=True)
            expo = jnp.exp(scores - peak)
            total = jnp.sum(expo, axis=1, keepdims=True)
            probs = (expo / total).astype(BF16)
            att[rows, lanes] = dot(probs, vo[:high, lanes], ((1,), (0,))).astype(BF16)
            lse[rows, lanes] = jnp.broadcast_to(peak + jnp.log(total), (block, HD))


def backward_kernel(block, q, k, v, g, lse, cos_ref, sin_ref, start_ref, dqo, dko, dvo, dq, dk, dv):
    length, width = q.shape
    dk[...] = jnp.zeros_like(dk)
    dv[...] = jnp.zeros_like(dv)
    for at in range(0, width, HD):
        lanes = slice(at, at + HD)
        for first in range(0, length, block):
            rows, high = slice(first, first + block), first + block
            query = q[rows, lanes] * BF16(HD**-0.5)
            key, grad = k[:high, lanes], g[rows, lanes]
            scores = masked_scores(query, key, start_ref[rows, :], first)
            probs = jnp.exp(scores - lse[rows, at : at + 1])
            dprob = dot(grad, v[:high, lanes], ((1,), (1,)))
            delta = jnp.sum(probs * dprob, axis=1, keepdims=True)
            draw = (probs * (dprob - delta)).astype(BF16)
            dq[rows, lanes] = dot(draw, key, ((1,), (0,))) * HD**-0.5
            dk[:high, lanes] += dot(draw, query, ((0,), (0,)))
            dv[:high, lanes] += dot(probs.astype(BF16), grad, ((0,), (0,)))
    cosine, sine = cos_ref[...], sin_ref[...]
    dqo[...] = (dq[...] * cosine - turn(dq[...] * sine)).astype(BF16)
    dko[...] = (dk[...] * cosine - turn(dk[...] * sine)).astype(BF16)
    dvo[...] = dv[...].astype(BF16)


def attention_specs(seqs, length, wide):
    lanes = min(128, wide)
    pairs = wide // lanes
    grid = (seqs, pairs)
    own = pl.BlockSpec((length, lanes), lambda s, p: (s, p))
    table = pl.BlockSpec((length, lanes), lambda s, p: (s, 0))
    starts = pl.BlockSpec((length, 1), lambda s, p: (s, 0))
    return grid, lanes, pairs, own, table, starts


def attend_forward(pre, cosine, sine, starts, seqs):
    rows, wide = pre.shape[0], pre.shape[1] // 3
    length = rows // seqs
    grid, lanes, pairs, own, table, start_spec = attention_specs(seqs, length, wide)
    if lanes == 128:
        parts = (pre, pre, pre)
        specs = [
            pl.BlockSpec((length, lanes), functools.partial(lambda c, s, p: (s, c * pairs + p), c))
            for c in range(3)
        ]
    else:
        parts = tuple(pre[:, c * wide : (c + 1) * wide] for c in range(3))
        specs = [own] * 3
    low = jax.ShapeDtypeStruct((rows, wide), BF16)
    return pl.pallas_call(
        functools.partial(forward_kernel, min(256, length)),
        grid=grid,
        in_specs=specs + [table, table, start_spec],
        out_specs=[own] * 5,
        out_shape=[low] * 4 + [jax.ShapeDtypeStruct((rows, wide), F32)],
        name="attend_forward",
    )(*parts, cosine, sine, starts)


def attend_backward(query, key, value, grad, lse, cosine, sine, starts, seqs):
    rows, wide = query.shape
    length = rows // seqs
    grid, lanes, pairs, own, table, start_spec = attention_specs(seqs, length, wide)
    low = jax.ShapeDtypeStruct((rows, wide), BF16)
    return pl.pallas_call(
        functools.partial(backward_kernel, min(256, length)),
        grid=grid,
        in_specs=[own] * 5 + [table, table, start_spec],
        out_specs=[own] * 3,
        out_shape=[low] * 3,
        scratch_shapes=[pltpu.VMEM((length, lanes), F32)] * 3,
        name="attend_backward",
    )(query, key, value, grad, lse, cosine, sine, starts)


def gather_in(weight):
    return lax.all_gather(weight, "gx", axis=0, tiled=True)


def gather_out(weight):
    whole = lax.all_gather(weight, "gx", axis=0)
    return jnp.swapaxes(whole, 0, 1).reshape(weight.shape[0], -1)


def grad_in(rows, grad):
    part = dot(rows, grad, ((0,), (0,))).astype(BF16)
    return lax.psum_scatter(part, "gx", scatter_dimension=0, tiled=True).astype(F32)


def grad_out_of(cols, grad):
    gx = lax.axis_size("gx")
    width = grad.shape[1] // gx
    parts = [
        dot(cols, grad[:, a * width : (a + 1) * width], ((0,), (0,))).astype(BF16)
        for a in range(gx)
    ]
    return lax.psum_scatter(jnp.stack(parts), "gx", scatter_dimension=0, tiled=False).astype(F32)


IN = ((1,), (0,))
BACK = ((1,), (1,))


def per_device(tokens, gain_attn, w_qkv, w_out, gain_mlp, w_gate_up, w_down, segments, grad_output):
    seqs, length = segments.shape
    wide = w_qkv.shape[2]
    width = w_down.shape[0]

    gains = lax.all_gather(jnp.stack([gain_attn, gain_mlp]), "gx", axis=1, tiled=True)
    wq = gather_in(w_qkv.reshape(w_qkv.shape[0], -1))
    wo = gather_out(w_out)
    wgu = gather_in(w_gate_up.reshape(w_gate_up.shape[0], -1))
    wd = gather_out(w_down)

    x = to_rows(tokens).astype(F32)
    dy_low = to_rows(grad_output)
    normed_a, scale_a = normalize(x, gains[0])
    rows_a = gather_rows(normed_a)
    dy_rows = gather_rows(dy_low)

    starts = doc_starts(segments)
    positions = jnp.arange(length, dtype=jnp.int32)[None, :] - starts
    cosine, sine = rotary(positions.reshape(-1), min(128, wide))
    starts = starts.reshape(-1, 1)

    pre = dot(rows_a, wq, IN)
    att, query, key, value, lse = attend_forward(pre, cosine, sine, starts, seqs)
    mid = x + project_sum(att, wo, IN)

    normed_m, scale_m = normalize(mid, gains[1])
    rows_m = gather_rows(normed_m)
    gate_up = dot(rows_m, wgu, IN)
    gate, up = gate_up[:, :width], gate_up[:, width:]
    sig = jax.nn.sigmoid(gate)
    hidden = (gate * sig * up).astype(BF16)
    grad_down = grad_out_of(hidden, dy_rows)
    dhid = dot(dy_rows, wd, BACK)
    dgate = dhid * up * sig * (1.0 + gate * (1.0 - sig))
    dup = dhid * gate * sig
    dgu = jnp.concatenate([dgate, dup], axis=1).astype(BF16)
    grad_gate_up = grad_in(rows_m, dgu)
    dnormed_m = project_sum(dgu, wgu, BACK)
    output = mid + project_sum(hidden, wd, IN)

    dmid_norm, gain_m = normalize_back(mid, gains[1], scale_m, dnormed_m)
    dmid = dy_low.astype(F32) + dmid_norm
    dmid_rows = gather_rows(dmid.astype(BF16))
    datt = dot(dmid_rows, wo, BACK).astype(BF16)
    grad_out = grad_out_of(att, dmid_rows)
    dpre = attend_backward(query, key, value, datt, lse, cosine, sine, starts, seqs)
    dpre = jnp.concatenate(dpre, axis=1)
    grad_qkv = grad_in(rows_a, dpre)
    dnormed_a = project_sum(dpre, wq, BACK)
    dx_norm, gain_a = normalize_back(x, gains[0], scale_a, dnormed_a)
    grad_tokens = dmid + dx_norm

    both = lax.psum(jnp.stack([gain_a, gain_m]), ("gx", "gy"))
    at = lax.axis_index("gx") * gain_attn.shape[0]
    both = lax.dynamic_slice_in_dim(both, at, gain_attn.shape[0], 1)
    return (
        to_blocks(output.astype(BF16)),
        to_blocks(grad_tokens.astype(BF16)).astype(F32),
        both[0],
        grad_qkv.reshape(w_qkv.shape),
        grad_out,
        both[1],
        grad_gate_up.reshape(w_gate_up.shape),
        grad_down,
    )


def solution(mesh):
    in_specs = (
        P("gy", "gx"),
        P("gx"),
        P("gx", None, "gy"),
        P("gy", "gx"),
        P("gx"),
        P("gx", None, "gy"),
        P("gy", "gx"),
        P("gx", None),
        P("gy", "gx"),
    )
    out_specs = (
        P("gy", "gx"),
        P("gy", "gx"),
        P("gx"),
        P("gx", None, "gy"),
        P("gy", "gx"),
        P("gx"),
        P("gx", None, "gy"),
        P("gy", "gx"),
    )
    return jax.shard_map(
        per_device, mesh=mesh, in_specs=in_specs, out_specs=out_specs, check_vma=False
    )
```

```python
import functools

import jax
import jax.numpy as jnp
from jax import lax
from jax.experimental import pallas as pl
from jax.experimental.pallas import tpu as pltpu
from jax.sharding import PartitionSpec as P


HD = 64
EPS = 1e-05
THETA = 130000.0
NEG = -1e30
BF16 = jnp.bfloat16
F32 = jnp.float32


def dot(left, right, dims):
    return lax.dot_general(left, right, (dims, ((), ())), preferred_element_type=F32)


def to_rows(block):
    gx, gy = lax.axis_size("gx"), lax.axis_size("gy")
    g = gy // gx
    i, j = lax.axis_index("gx"), lax.axis_index("gy")
    parts = block.reshape(gx, block.shape[0] // gx, block.shape[1])
    came = []
    for k in range(gx):
        perm = [
            (a * gy + s * g + r, s * gy + r * gx + (a + k) % gx)
            for a in range(gx)
            for s in range(gx)
            for r in range(g)
        ]
        part = lax.dynamic_index_in_dim(parts, (i + k) % gx, 0, keepdims=False)
        came.append(lax.ppermute(part, ("gx", "gy"), perm))
    q = j % gx
    return jnp.concatenate([lax.select_n((q - a) % gx, *came) for a in range(gx)], axis=1)


def to_blocks(rows):
    gx, gy = lax.axis_size("gx"), lax.axis_size("gy")
    g = gy // gx
    i, j = lax.axis_index("gx"), lax.axis_index("gy")
    q = j % gx
    width = rows.shape[1] // gx
    parts = [rows[:, a * width : (a + 1) * width] for a in range(gx)]
    came = []
    for k in range(gx):
        perm = [
            (s * gy + r * gx + (a + k) % gx, a * gy + s * g + r)
            for a in range(gx)
            for s in range(gx)
            for r in range(g)
        ]
        came.append(lax.ppermute(lax.select_n((q - k) % gx, *parts), ("gx", "gy"), perm))
    return jnp.concatenate([lax.select_n((b - i) % gx, *came) for b in range(gx)], axis=0)


def swap(value, bit):
    size = lax.axis_size("gy")
    return lax.ppermute(value, "gy", [(a, a ^ bit) for a in range(size)])


def mine(bit):
    return (lax.axis_index("gy") & bit) != 0


def joined(value, bit, axis):
    other = swap(value, bit)
    up = mine(bit)
    return jnp.stack([jnp.where(up, other, value), jnp.where(up, value, other)], axis=axis)


def gather_rows(rows):
    if lax.axis_size("gy") != 8:
        return lax.all_gather(rows, "gy", axis=0, tiled=True)
    n, width = rows.shape
    half = width // 2
    left, right = rows[:, :half], rows[:, half:]
    left = joined(joined(left, 2, 0), 4, 0)
    right = joined(joined(right, 4, 0), 2, 1)
    both = [joined(v.reshape(4, n, half), 1, 1).reshape(8 * n, half) for v in (left, right)]
    return jnp.concatenate(both, axis=1)


def halves(value, bit, axis):
    up = mine(bit)
    low, high = lax.index_in_dim(value, 0, axis, False), lax.index_in_dim(value, 1, axis, False)
    return jnp.where(up, high, low), jnp.where(up, low, high)


def reduced(value, bit, axis):
    keep, send = halves(value, bit, axis)
    return keep.astype(F32) + swap(send.astype(BF16), bit).astype(F32)


def project_sum(left, weight, dims):
    if lax.axis_size("gy") != 8:
        part = dot(left, weight, dims).astype(BF16)
        return lax.psum_scatter(part, "gy", scatter_dimension=0, tiled=True).astype(F32)
    n = left.shape[0] // 8
    keep, send = halves(left.reshape(4, 2, n, left.shape[1]), 1, 1)
    other = swap(dot(send.reshape(4 * n, -1), weight, dims).astype(BF16), 1)
    total = dot(keep.reshape(4 * n, -1), weight, dims) + other.astype(F32)
    total = total.reshape(2, 2, n, -1)
    half = total.shape[3] // 2
    left_half = reduced(reduced(total[..., :half], 4, 0), 2, 0)
    right_half = reduced(reduced(total[..., half:], 2, 1), 4, 0)
    return jnp.concatenate([left_half, right_half], axis=1)


def whole_width(local):
    gx = lax.axis_size("gx")
    i = lax.axis_index("gx")
    came = [local] + [
        lax.ppermute(local, "gx", [(a, (a + k) % gx) for a in range(gx)]) for k in range(1, gx)
    ]
    return jnp.concatenate([lax.select_n((i - a) % gx, *came) for a in range(gx)], axis=-1)


def sum_width(parts):
    gx, gy = lax.axis_size("gx"), lax.axis_size("gy")
    i = lax.axis_index("gx")
    width = parts.shape[-1] // gx
    blocks = [parts[..., a * width : (a + 1) * width] for a in range(gx)]
    total = lax.select_n(i, *blocks)
    for k in range(1, gx):
        send = lax.select_n((i + k) % gx, *blocks)
        total = total + lax.ppermute(send, "gx", [(a, (a + k) % gx) for a in range(gx)])
    bit = 1
    while bit < gy:
        total = total + swap(total, bit)
        bit *= 2
    return total


def after(value, *first):
    return lax.optimization_barrier((value,) + first)[0]


def normalize(value, gain):
    scale = lax.rsqrt(jnp.mean(value * value, axis=1, keepdims=True) + EPS)
    return (value * scale * gain[None, :]).astype(BF16), scale


def normalize_back(value, gain, scale, grad):
    weighted = grad * gain[None, :]
    inner = jnp.mean(weighted * value, axis=1, keepdims=True)
    grad_gain = jnp.sum(grad * value * scale, axis=0)
    return scale * weighted - value * (scale * scale * scale * inner), grad_gain


def doc_starts(segs):
    index = jnp.broadcast_to(jnp.arange(segs.shape[1], dtype=jnp.int32)[None, :], segs.shape)
    before = jnp.concatenate([segs[:, :1] - 1, segs[:, :-1]], axis=1)
    return lax.cummax(jnp.where(segs != before, index, jnp.zeros_like(index)), axis=1)


def rotary(positions, width):
    half = HD // 2
    freq = THETA ** (-jnp.arange(half, dtype=F32) * 2.0 / HD)
    angle = positions.astype(F32)[:, None] * freq[None, :]
    copies = width // half
    return jnp.tile(jnp.cos(angle), (1, copies)), jnp.tile(jnp.sin(angle), (1, copies))


def turn(value):
    width = value.shape[1]
    half = HD // 2
    pieces = []
    for at in range(0, width, HD):
        pieces += [-value[:, at + half : at + HD], value[:, at : at + half]]
    return jnp.concatenate(pieces, axis=1)


def masked_scores(query, key, start, first):
    scores = dot(query, key, ((1,), (1,)))
    kidx = lax.broadcasted_iota(jnp.int32, scores.shape, 1)
    qidx = lax.broadcasted_iota(jnp.int32, scores.shape, 0) + first
    return jnp.where((kidx >= start) & (kidx <= qidx), scores, NEG)


def forward_kernel(block, q_ref, k_ref, v_ref, cos_ref, sin_ref, start_ref, att, qo, ko, vo, lse):
    cosine, sine = cos_ref[...], sin_ref[...]
    q, k = q_ref[...], k_ref[...]
    qo[...] = (q * cosine + turn(q) * sine).astype(BF16)
    ko[...] = (k * cosine + turn(k) * sine).astype(BF16)
    vo[...] = v_ref[...].astype(BF16)
    length, width = q.shape
    for at in range(0, width, HD):
        lanes = slice(at, at + HD)
        for first in range(0, length, block):
            rows, high = slice(first, first + block), first + block
            query = qo[rows, lanes] * BF16(HD**-0.5)
            scores = masked_scores(query, ko[:high, lanes], start_ref[rows, :], first)
            peak = jnp.max(scores, axis=1, keepdims=True)
            expo = jnp.exp(scores - peak)
            total = jnp.sum(expo, axis=1, keepdims=True)
            probs = (expo / total).astype(BF16)
            att[rows, lanes] = dot(probs, vo[:high, lanes], ((1,), (0,))).astype(BF16)
            lse[rows, lanes] = jnp.broadcast_to(peak + jnp.log(total), (block, HD))


def backward_kernel(block, q, k, v, g, lse, cos_ref, sin_ref, start_ref, dqo, dko, dvo, dq, dk, dv):
    length, width = q.shape
    dk[...] = jnp.zeros_like(dk)
    dv[...] = jnp.zeros_like(dv)
    for at in range(0, width, HD):
        lanes = slice(at, at + HD)
        for first in range(0, length, block):
            rows, high = slice(first, first + block), first + block
            query = q[rows, lanes] * BF16(HD**-0.5)
            key, grad = k[:high, lanes], g[rows, lanes]
            scores = masked_scores(query, key, start_ref[rows, :], first)
            probs = jnp.exp(scores - lse[rows, at : at + 1])
            dprob = dot(grad, v[:high, lanes], ((1,), (1,)))
            delta = jnp.sum(probs * dprob, axis=1, keepdims=True)
            draw = (probs * (dprob - delta)).astype(BF16)
            dq[rows, lanes] = dot(draw, key, ((1,), (0,))) * HD**-0.5
            dk[:high, lanes] += dot(draw, query, ((0,), (0,)))
            dv[:high, lanes] += dot(probs.astype(BF16), grad, ((0,), (0,)))
    cosine, sine = cos_ref[...], sin_ref[...]
    dqo[...] = (dq[...] * cosine - turn(dq[...] * sine)).astype(BF16)
    dko[...] = (dk[...] * cosine - turn(dk[...] * sine)).astype(BF16)
    dvo[...] = dv[...].astype(BF16)


def attention_specs(seqs, length, wide):
    lanes = min(128, wide)
    pairs = wide // lanes
    grid = (seqs, pairs)
    own = pl.BlockSpec((length, lanes), lambda s, p: (s, p))
    table = pl.BlockSpec((length, lanes), lambda s, p: (s, 0))
    starts = pl.BlockSpec((length, 1), lambda s, p: (s, 0))
    return grid, lanes, pairs, own, table, starts


def attend_forward(pre, cosine, sine, starts, seqs):
    rows, wide = pre.shape[0], pre.shape[1] // 3
    length = rows // seqs
    grid, lanes, pairs, own, table, start_spec = attention_specs(seqs, length, wide)
    if lanes == 128:
        parts = (pre, pre, pre)
        specs = [
            pl.BlockSpec((length, lanes), functools.partial(lambda c, s, p: (s, c * pairs + p), c))
            for c in range(3)
        ]
    else:
        parts = tuple(pre[:, c * wide : (c + 1) * wide] for c in range(3))
        specs = [own] * 3
    low = jax.ShapeDtypeStruct((rows, wide), BF16)
    return pl.pallas_call(
        functools.partial(forward_kernel, min(256, length)),
        grid=grid,
        in_specs=specs + [table, table, start_spec],
        out_specs=[own] * 5,
        out_shape=[low] * 4 + [jax.ShapeDtypeStruct((rows, wide), F32)],
        name="attend_forward",
    )(*parts, cosine, sine, starts)


def attend_backward(query, key, value, grad, lse, cosine, sine, starts, seqs):
    rows, wide = query.shape
    length = rows // seqs
    grid, lanes, _, own, table, start_spec = attention_specs(seqs, length, wide)
    low = jax.ShapeDtypeStruct((rows, wide), BF16)
    return pl.pallas_call(
        functools.partial(backward_kernel, min(256, length)),
        grid=grid,
        in_specs=[own] * 5 + [table, table, start_spec],
        out_specs=[own] * 3,
        out_shape=[low] * 3,
        scratch_shapes=[pltpu.VMEM((length, lanes), F32)] * 3,
        name="attend_backward",
    )(query, key, value, grad, lse, cosine, sine, starts)


def gather_in(weight):
    return lax.all_gather(weight, "gx", axis=0, tiled=True)


def gather_out(weight):
    whole = lax.all_gather(weight, "gx", axis=0)
    return jnp.swapaxes(whole, 0, 1).reshape(weight.shape[0], -1)


def grad_in(rows, grad):
    return dot(rows, grad, ((0,), (0,))).astype(BF16)


def sum_in(part):
    return lax.psum_scatter(part, "gx", scatter_dimension=0, tiled=True).astype(F32)


def grad_out_of(cols, grad):
    gx = lax.axis_size("gx")
    width = grad.shape[1] // gx
    parts = [
        dot(cols, grad[:, a * width : (a + 1) * width], ((0,), (0,))).astype(BF16)
        for a in range(gx)
    ]
    return jnp.stack(parts)


def sum_out(part):
    return lax.psum_scatter(part, "gx", scatter_dimension=0, tiled=False).astype(F32)


IN = ((1,), (0,))
BACK = ((1,), (1,))


def layer(tokens, gain_attn, w_qkv, w_out, gain_mlp, w_gate_up, w_down, segments, grad_output):
    seqs, length = segments.shape
    wide = w_qkv.shape[2]
    width = w_down.shape[0]

    wq = gather_in(w_qkv.reshape(w_qkv.shape[0], -1))
    wo = gather_out(w_out)
    wgu = gather_in(w_gate_up.reshape(w_gate_up.shape[0], -1))
    wd = gather_out(w_down)

    x = to_rows(tokens).astype(F32)
    gains = whole_width(jnp.stack([gain_attn, gain_mlp]))
    normed_a, scale_a = normalize(x, gains[0])
    rows_a = gather_rows(normed_a)
    dy_low = to_rows(grad_output)
    dy_rows = gather_rows(dy_low)

    starts = doc_starts(segments)
    positions = jnp.arange(length, dtype=jnp.int32)[None, :] - starts
    cosine, sine = rotary(positions.reshape(-1), min(128, wide))
    starts = starts.reshape(-1, 1)

    rows_a = after(rows_a, dy_rows, cosine, sine)
    pre = dot(rows_a, wq, IN)
    att, query, key, value, lse = attend_forward(pre, cosine, sine, starts, seqs)
    mid = x + project_sum(att, wo, IN)

    normed_m, scale_m = normalize(mid, gains[1])
    rows_m = gather_rows(normed_m)
    gate_up = dot(rows_m, wgu, IN)
    gate, up = gate_up[:, :width], gate_up[:, width:]
    sig = jax.nn.sigmoid(gate)
    hidden = (gate * sig * up).astype(BF16)
    down_part = grad_out_of(hidden, dy_rows)
    dhid = dot(after(dy_rows, down_part), wd, BACK)
    dgate = dhid * up * sig * (1.0 + gate * (1.0 - sig))
    dup = dhid * gate * sig
    dgu = jnp.concatenate([dgate, dup], axis=1).astype(BF16)
    gate_up_part = grad_in(rows_m, dgu)
    dgu = after(dgu, gate_up_part)
    dnormed_m = project_sum(dgu, wgu, BACK)

    dmid_norm, gain_m = normalize_back(mid, gains[1], scale_m, dnormed_m)
    dmid = dy_low.astype(F32) + dmid_norm
    dmid_rows = gather_rows(dmid.astype(BF16))
    out_part = grad_out_of(att, dmid_rows)
    datt = dot(after(dmid_rows, out_part), wo, BACK).astype(BF16)
    dpre = attend_backward(query, key, value, datt, lse, cosine, sine, starts, seqs)
    dpre = jnp.concatenate(dpre, axis=1)
    qkv_part = grad_in(rows_a, dpre)
    dnormed_a = project_sum(after(dpre, qkv_part), wq, BACK)
    dx_norm, gain_a = normalize_back(x, gains[0], scale_a, dnormed_a)
    grad_tokens = to_blocks((dmid + dx_norm).astype(BF16)).astype(F32)
    gain_a = sum_width(gain_a)
    output = mid + project_sum(after(hidden, dnormed_a), wd, IN)

    return (
        to_blocks(output.astype(BF16)),
        grad_tokens,
        gain_a,
        sum_in(qkv_part).reshape(w_qkv.shape),
        sum_out(out_part),
        sum_width(gain_m),
        sum_in(gate_up_part).reshape(w_gate_up.shape),
        sum_out(down_part),
    )


def solution(mesh):
    in_specs = (
        P("gy", "gx"),
        P("gx"),
        P("gx", None, "gy"),
        P("gy", "gx"),
        P("gx"),
        P("gx", None, "gy"),
        P("gy", "gx"),
        P("gx", None),
        P("gy", "gx"),
    )
    out_specs = (
        P("gy", "gx"),
        P("gy", "gx"),
        P("gx"),
        P("gx", None, "gy"),
        P("gy", "gx"),
        P("gx"),
        P("gx", None, "gy"),
        P("gy", "gx"),
    )
    return jax.shard_map(layer, mesh=mesh, in_specs=in_specs, out_specs=out_specs, check_vma=False)
```

```python
import functools

import jax
import jax.numpy as jnp
from jax import lax
from jax.experimental import pallas as pl
from jax.experimental.pallas import tpu as pltpu
from jax.sharding import PartitionSpec as P


HD = 64
EPS = 1e-05
THETA = 130000.0
NEG = -1e30
BF16 = jnp.bfloat16
F32 = jnp.float32


def dot(left, right, dims):
    return lax.dot_general(left, right, (dims, ((), ())), preferred_element_type=F32)


def swap(value, k, axis="gy"):
    return lax.ppermute(value, axis, [(a, a ^ k) for a in range(lax.axis_size(axis))])


def at(values, index):
    if isinstance(values, list):
        values = jnp.stack(values)
    return lax.dynamic_index_in_dim(values, index, 0, keepdims=False)


def pick(values, index):
    return lax.select_n(index, *values)


def columns():
    gx, gy = lax.axis_size("gx"), lax.axis_size("gy")
    g = gy // gx
    return gx, g, lax.axis_index("gx"), lax.axis_index("gy") // g


def to_rows(block):
    gx, g, i, s = columns()
    many, rows, width = block.shape
    parts = jnp.swapaxes(block.reshape(many, gx, rows // gx, width), 0, 1)
    came = [at(parts, s)] + [swap(at(parts, s ^ k), k * g) for k in range(1, gx)]
    came = jnp.stack(came)
    came = [at(came, i ^ s)] + [swap(at(came, i ^ k ^ s), k, "gx") for k in range(1, gx)]
    return jnp.concatenate([pick(came, a ^ i) for a in range(gx)], axis=2)


def to_blocks(rows):
    gx, g, i, q = columns()
    width = rows.shape[1] // gx
    parts = [rows[:, a * width : (a + 1) * width] for a in range(gx)]
    came = [pick(parts, i)] + [swap(pick(parts, i ^ k), k, "gx") for k in range(1, gx)]
    came = jnp.stack(came)
    came = [at(came, q ^ i)] + [swap(at(came, q ^ k ^ i), k * g) for k in range(1, gx)]
    return jnp.concatenate([pick(came, a ^ q) for a in range(gx)], axis=0)


def joined(value, bit, spot, axis="gy"):
    other = swap(value, bit, axis)
    up = (lax.axis_index(axis) & bit) != 0
    both = jnp.stack([value, value], axis=spot)
    return lax.dynamic_update_index_in_dim(both, other, jnp.where(up, 0, 1), spot)


def gather_rows(rows, pair=False):
    gx, g = lax.axis_size("gx"), lax.axis_size("gy") // lax.axis_size("gx")
    if pair:
        rows = joined(rows, 1, 0, "gx").reshape(-1, rows.shape[1])
    n, width = rows.shape
    if lax.axis_size("gy") != 8:
        whole = lax.all_gather(rows, "gy", axis=0, tiled=True).reshape(gx, g, n, width)
        return jnp.swapaxes(whole, 0, 1).reshape(-1, width)
    half = width // 2
    left, right = rows[:, :half], rows[:, half:]
    left = joined(joined(left, 2, 0), 4, 0)
    right = joined(joined(right, 4, 0), 2, 1)
    both = [joined(v.reshape(4 * n, half), 1, 0).reshape(8 * n, half) for v in (left, right)]
    return jnp.concatenate(both, axis=1)


def reduced(value, bit, spot, axis="gy"):
    up = jnp.where((lax.axis_index(axis) & bit) != 0, 1, 0)
    send = lax.dynamic_index_in_dim(value, 1 - up, spot, keepdims=False).astype(BF16)
    keep = lax.dynamic_index_in_dim(value, up, spot, keepdims=False)
    return keep + swap(send, bit, axis).astype(F32)


def project_sum(left, weight, dims, pair=False):
    gx, g = lax.axis_size("gx"), lax.axis_size("gy") // lax.axis_size("gx")
    n = left.shape[0] // (gx * g)
    if lax.axis_size("gy") != 8:
        left = jnp.swapaxes(left.reshape(g, gx, n, -1), 0, 1).reshape(left.shape)
        part = dot(left, weight, dims).astype(BF16)
        total = lax.psum_scatter(part, "gy", scatter_dimension=0, tiled=True).astype(F32)
    else:
        up = lax.axis_index("gy") & 1
        left = left.reshape(2, 4 * n, -1)
        other = swap(dot(at(left, 1 - up), weight, dims).astype(BF16), 1)
        total = dot(at(left, up), weight, dims) + other.astype(F32)
        total = total.reshape(2, 2, n, -1)
        half = total.shape[3] // 2
        left_half = reduced(reduced(total[..., :half], 4, 0), 2, 0)
        right_half = reduced(reduced(total[..., half:], 2, 1), 4, 0)
        total = jnp.concatenate([left_half, right_half], axis=1)
    if pair:
        total = reduced(total.reshape(2, n // 2, -1), 1, 0, "gx")
    return total


def whole_width(local):
    gx = lax.axis_size("gx")
    i = lax.axis_index("gx")
    came = [local] + [
        lax.ppermute(local, "gx", [(a, (a + k) % gx) for a in range(gx)]) for k in range(1, gx)
    ]
    return jnp.concatenate([lax.select_n((i - a) % gx, *came) for a in range(gx)], axis=-1)


def sum_width(parts):
    gx, gy = lax.axis_size("gx"), lax.axis_size("gy")
    i = lax.axis_index("gx")
    width = parts.shape[-1] // gx
    blocks = [parts[..., a * width : (a + 1) * width] for a in range(gx)]
    total = lax.select_n(i, *blocks)
    for k in range(1, gx):
        send = lax.select_n((i + k) % gx, *blocks)
        total = total + lax.ppermute(send, "gx", [(a, (a + k) % gx) for a in range(gx)])
    bit = 1
    while bit < gy:
        total = total + swap(total, bit)
        bit *= 2
    return total


def after(value, *first):
    return lax.optimization_barrier((value,) + first)[0]


def normalize(value, gain):
    scale = lax.rsqrt(jnp.mean(value * value, axis=1, keepdims=True) + EPS)
    return (value * scale * gain[None, :]).astype(BF16), scale


def normalize_back(value, gain, scale, grad):
    weighted = grad * gain[None, :]
    inner = jnp.mean(weighted * value, axis=1, keepdims=True)
    grad_gain = jnp.sum(grad * value * scale, axis=0)
    return scale * weighted - value * (scale * scale * scale * inner), grad_gain


def doc_starts(segs):
    index = jnp.broadcast_to(jnp.arange(segs.shape[1], dtype=jnp.int32)[None, :], segs.shape)
    before = jnp.concatenate([segs[:, :1] - 1, segs[:, :-1]], axis=1)
    return lax.cummax(jnp.where(segs != before, index, jnp.zeros_like(index)), axis=1)


def rotary(positions, width):
    half = HD // 2
    freq = THETA ** (-jnp.arange(half, dtype=F32) * 2.0 / HD)
    angle = positions.astype(F32)[:, None] * freq[None, :]
    copies = width // half
    return jnp.tile(jnp.cos(angle), (1, copies)), jnp.tile(jnp.sin(angle), (1, copies))


def turn(value):
    width = value.shape[1]
    half = HD // 2
    pieces = []
    for at in range(0, width, HD):
        pieces += [-value[:, at + half : at + HD], value[:, at : at + half]]
    return jnp.concatenate(pieces, axis=1)


def masked_scores(query, key, start, first):
    scores = dot(query, key, ((1,), (1,)))
    kidx = lax.broadcasted_iota(jnp.int32, scores.shape, 1)
    qidx = lax.broadcasted_iota(jnp.int32, scores.shape, 0) + first
    return jnp.where((kidx >= start) & (kidx <= qidx), scores, NEG)


def forward_kernel(block, q_ref, k_ref, v_ref, cos_ref, sin_ref, start_ref, att, qo, ko, vo, lse):
    cosine, sine = cos_ref[...], sin_ref[...]
    q, k = q_ref[...], k_ref[...]
    qo[...] = (q * cosine + turn(q) * sine).astype(BF16)
    ko[...] = (k * cosine + turn(k) * sine).astype(BF16)
    vo[...] = v_ref[...].astype(BF16)
    length, width = q.shape
    for at in range(0, width, HD):
        lanes = slice(at, at + HD)
        for first in range(0, length, block):
            rows, high = slice(first, first + block), first + block
            query = qo[rows, lanes] * BF16(HD**-0.5)
            scores = masked_scores(query, ko[:high, lanes], start_ref[rows, :], first)
            peak = jnp.max(scores, axis=1, keepdims=True)
            expo = jnp.exp(scores - peak)
            total = jnp.sum(expo, axis=1, keepdims=True)
            probs = (expo / total).astype(BF16)
            att[rows, lanes] = dot(probs, vo[:high, lanes], ((1,), (0,))).astype(BF16)
            lse[rows, lanes] = jnp.broadcast_to(peak + jnp.log(total), (block, HD))


def backward_kernel(block, q, k, v, g, lse, cos_ref, sin_ref, start_ref, dqo, dko, dvo, dq, dk, dv):
    length, width = q.shape
    dk[...] = jnp.zeros_like(dk)
    dv[...] = jnp.zeros_like(dv)
    for at in range(0, width, HD):
        lanes = slice(at, at + HD)
        for first in range(0, length, block):
            rows, high = slice(first, first + block), first + block
            query = q[rows, lanes] * BF16(HD**-0.5)
            key, grad = k[:high, lanes], g[rows, lanes]
            scores = masked_scores(query, key, start_ref[rows, :], first)
            probs = jnp.exp(scores - lse[rows, at : at + 1])
            dprob = dot(grad, v[:high, lanes], ((1,), (1,)))
            delta = jnp.sum(probs * dprob, axis=1, keepdims=True)
            draw = (probs * (dprob - delta)).astype(BF16)
            dq[rows, lanes] = dot(draw, key, ((1,), (0,))) * HD**-0.5
            dk[:high, lanes] += dot(draw, query, ((0,), (0,)))
            dv[:high, lanes] += dot(probs.astype(BF16), grad, ((0,), (0,)))
    cosine, sine = cos_ref[...], sin_ref[...]
    dqo[...] = (dq[...] * cosine - turn(dq[...] * sine)).astype(BF16)
    dko[...] = (dk[...] * cosine - turn(dk[...] * sine)).astype(BF16)
    dvo[...] = dv[...].astype(BF16)


def attention_specs(seqs, length, wide):
    lanes = min(128, wide)
    pairs = wide // lanes
    grid = (seqs, pairs)
    own = pl.BlockSpec((length, lanes), lambda s, p: (s, p))
    table = pl.BlockSpec((length, lanes), lambda s, p: (s, 0))
    starts = pl.BlockSpec((length, 1), lambda s, p: (s, 0))
    return grid, lanes, pairs, own, table, starts


def attend_forward(pre, cosine, sine, starts, seqs):
    rows, wide = pre.shape[0], pre.shape[1] // 3
    length = rows // seqs
    grid, lanes, pairs, own, table, start_spec = attention_specs(seqs, length, wide)
    if lanes == 128:
        parts = (pre, pre, pre)
        specs = [
            pl.BlockSpec((length, lanes), functools.partial(lambda c, s, p: (s, c * pairs + p), c))
            for c in range(3)
        ]
    else:
        parts = tuple(pre[:, c * wide : (c + 1) * wide] for c in range(3))
        specs = [own] * 3
    low = jax.ShapeDtypeStruct((rows, wide), BF16)
    return pl.pallas_call(
        functools.partial(forward_kernel, min(256, length)),
        grid=grid,
        in_specs=specs + [table, table, start_spec],
        out_specs=[own] * 5,
        out_shape=[low] * 4 + [jax.ShapeDtypeStruct((rows, wide), F32)],
        name="attend_forward",
    )(*parts, cosine, sine, starts)


def attend_backward(query, key, value, grad, lse, cosine, sine, starts, seqs):
    rows, wide = query.shape
    length = rows // seqs
    grid, lanes, _, own, table, start_spec = attention_specs(seqs, length, wide)
    low = jax.ShapeDtypeStruct((rows, wide), BF16)
    return pl.pallas_call(
        functools.partial(backward_kernel, min(256, length)),
        grid=grid,
        in_specs=[own] * 5 + [table, table, start_spec],
        out_specs=[own] * 3,
        out_shape=[low] * 3,
        scratch_shapes=[pltpu.VMEM((length, lanes), F32)] * 3,
        name="attend_backward",
    )(query, key, value, grad, lse, cosine, sine, starts)


def gather_in(weight):
    return lax.all_gather(weight, "gx", axis=0, tiled=True)


def gather_out(weight):
    whole = lax.all_gather(weight, "gx", axis=0)
    return jnp.swapaxes(whole, 0, 1).reshape(weight.shape[0], -1)


def sum_in(part):
    return lax.psum_scatter(part, "gx", scatter_dimension=0, tiled=True).astype(F32)


def grad_out_of(cols, grad):
    gx = lax.axis_size("gx")
    width = grad.shape[1] // gx
    parts = [
        dot(cols, grad[:, a * width : (a + 1) * width], ((0,), (0,))).astype(BF16)
        for a in range(gx)
    ]
    return jnp.stack(parts)


def sum_out(part):
    return lax.psum_scatter(part, "gx", scatter_dimension=0, tiled=False).astype(F32)


def halves_from_planes(low, high, spot):
    gx, i = lax.axis_size("gx"), lax.axis_index("gx")
    odd = i & 1
    own, other = pick([low, high], odd), pick([high, low], odd)
    size = own.shape[spot]
    whole = jnp.concatenate([own] * gx, axis=spot)
    for k in range(1, gx):
        came = swap(other if k & 1 else own, k, "gx")
        whole = lax.dynamic_update_slice_in_dim(whole, came, (i ^ k) * size, spot)
    return whole


def halves_to_planes(part, spot):
    gx, i = lax.axis_size("gx"), lax.axis_index("gx")
    odd = i & 1
    size = part.shape[spot] // gx
    own = lax.dynamic_slice_in_dim(part, i * size, size, spot).astype(F32)
    other = None
    for k in range(1, gx):
        send = lax.dynamic_slice_in_dim(part, (i ^ k) * size, size, spot)
        came = swap(send, k, "gx").astype(F32)
        if k & 1:
            other = came if other is None else other + came
        else:
            own = own + came
    return pick([own, other], odd), pick([other, own], odd)


IN = ((1,), (0,))
BACK = ((1,), (1,))
TOKENS = ((0,), (0,))


def layer(tokens, gain_attn, w_qkv, w_out, gain_mlp, w_gate_up, w_down, segments, grad_output):
    seqs, length = segments.shape
    wide = w_qkv.shape[2]
    width = w_down.shape[0] // 2

    wq = gather_in(w_qkv.reshape(w_qkv.shape[0], -1))
    wo = gather_out(w_out)

    x, dy_low = to_rows(jnp.stack([tokens, grad_output]))
    x = x.astype(F32)
    gains = whole_width(jnp.stack([gain_attn, gain_mlp]))
    normed_a, scale_a = normalize(x, gains[0])
    rows_a = gather_rows(normed_a)

    starts = doc_starts(segments)
    positions = jnp.arange(length, dtype=jnp.int32)[None, :] - starts
    cosine, sine = rotary(positions.reshape(-1), min(128, wide))
    starts = starts.reshape(-1, 1)

    rows_a = after(rows_a, cosine, sine)
    pre = dot(rows_a, wq, IN)
    gu_low = jnp.concatenate([w_gate_up[:, 0, :width], w_gate_up[:, 1, :width]], axis=1)
    gu_high = jnp.concatenate([w_gate_up[:, 0, width:], w_gate_up[:, 1, width:]], axis=1)
    gu_low, gu_high, dy_low = after((gu_low, gu_high, dy_low), wq)
    wgu = halves_from_planes(gu_low, gu_high, 0)
    dy_rows = gather_rows(dy_low, True)

    att, query, key, value, lse = attend_forward(pre, cosine, sine, starts, seqs)
    down = after(w_down, att)
    wd = halves_from_planes(down[:width], down[width:], 1)
    mid = x + project_sum(att, wo, IN)

    normed_m, scale_m = normalize(mid, gains[1])
    rows_m = gather_rows(normed_m, True)
    gate_up = dot(rows_m, wgu, IN)
    gate, up = gate_up[:, :width], gate_up[:, width:]
    sig = jax.nn.sigmoid(gate)
    hidden = (gate * sig * up).astype(BF16)
    down_part = dot(hidden, dy_rows, TOKENS).astype(BF16)
    dhid = dot(after(dy_rows, down_part), wd, BACK)
    dgate = dhid * up * sig * (1.0 + gate * (1.0 - sig))
    dup = dhid * gate * sig
    dgu = jnp.concatenate([dgate, dup], axis=1).astype(BF16)
    gate_up_part = dot(rows_m, dgu, TOKENS).astype(BF16)
    dnormed_m = project_sum(after(dgu, gate_up_part), wgu, BACK, True)

    dmid_norm, gain_m = normalize_back(mid, gains[1], scale_m, dnormed_m)
    dmid = dy_low.astype(F32) + dmid_norm
    dmid_rows = gather_rows(dmid.astype(BF16))
    out_part = grad_out_of(att, dmid_rows)
    datt = dot(after(dmid_rows, out_part), wo, BACK).astype(BF16)
    dpre = attend_backward(query, key, value, datt, lse, cosine, sine, starts, seqs)
    dpre = jnp.concatenate(dpre, axis=1)
    qkv_part = dot(rows_a, dpre, TOKENS).astype(BF16)
    dnormed_a = project_sum(after(dpre, qkv_part), wq, BACK)
    dx_norm, gain_a = normalize_back(x, gains[0], scale_a, dnormed_a)
    grad_tokens = to_blocks((dmid + dx_norm).astype(BF16)).astype(F32)
    output = mid + project_sum(after(hidden, datt), wd, IN, True)

    down_low, down_high = halves_to_planes(down_part, 1)
    gu_low, gu_high = halves_to_planes(gate_up_part, 0)
    grad_gate_up = jnp.stack(
        [
            jnp.concatenate([gu_low[:, at : at + width], gu_high[:, at : at + width]], axis=1)
            for at in (0, width)
        ],
        axis=1,
    )
    return (
        to_blocks(output.astype(BF16)),
        grad_tokens,
        sum_width(gain_a),
        sum_in(qkv_part).reshape(w_qkv.shape),
        sum_out(out_part),
        sum_width(gain_m),
        grad_gate_up,
        jnp.concatenate([down_low, down_high], axis=0),
    )


def solution(mesh):
    in_specs = (
        P("gy", "gx"),
        P("gx"),
        P("gx", None, "gy"),
        P("gy", "gx"),
        P("gx"),
        P("gx", None, "gy"),
        P("gy", "gx"),
        P("gx", None),
        P("gy", "gx"),
    )
    out_specs = (
        P("gy", "gx"),
        P("gy", "gx"),
        P("gx"),
        P("gx", None, "gy"),
        P("gy", "gx"),
        P("gx"),
        P("gx", None, "gy"),
        P("gy", "gx"),
    )
    return jax.shard_map(layer, mesh=mesh, in_specs=in_specs, out_specs=out_specs, check_vma=False)
```

```python
import functools

import jax
import jax.numpy as jnp
from jax import lax
from jax.experimental import pallas as pl
from jax.experimental.pallas import tpu as pltpu
from jax.sharding import PartitionSpec as P


HD = 64
EPS = 1e-05
THETA = 130000.0
NEG = -1e30
BF16 = jnp.bfloat16
F32 = jnp.float32


def dot(left, right, dims):
    return lax.dot_general(left, right, (dims, ((), ())), preferred_element_type=F32)


def swap(value, k, axis="gy"):
    return lax.ppermute(value, axis, [(a, a ^ k) for a in range(lax.axis_size(axis))])


def at(values, index):
    if isinstance(values, list):
        values = jnp.stack(values)
    return lax.dynamic_index_in_dim(values, index, 0, keepdims=False)


def pick(values, index):
    return lax.select_n(index, *values)


def columns():
    gx, gy = lax.axis_size("gx"), lax.axis_size("gy")
    g = gy // gx
    return gx, g, lax.axis_index("gx"), lax.axis_index("gy") // g


def to_rows(block):
    gx, g, i, s = columns()
    parts = block.reshape(gx, block.shape[0] // gx, block.shape[1])
    came = [at(parts, s)] + [swap(at(parts, s ^ k), k * g) for k in range(1, gx)]
    came = jnp.stack(came)
    came = [at(came, i ^ s)] + [swap(at(came, i ^ k ^ s), k, "gx") for k in range(1, gx)]
    return jnp.concatenate([pick(came, a ^ i) for a in range(gx)], axis=1)


def to_blocks(rows):
    gx, g, i, q = columns()
    width = rows.shape[1] // gx
    parts = [rows[:, a * width : (a + 1) * width] for a in range(gx)]
    came = [pick(parts, i)] + [swap(pick(parts, i ^ k), k, "gx") for k in range(1, gx)]
    came = jnp.stack(came)
    came = [at(came, q ^ i)] + [swap(at(came, q ^ k ^ i), k * g) for k in range(1, gx)]
    return jnp.concatenate([pick(came, a ^ q) for a in range(gx)], axis=0)


def joined(value, bit, spot, axis="gy"):
    return joined_with(value, swap(value, bit, axis), bit, spot, axis)


def joined_with(value, other, bit, spot, axis):
    up = (lax.axis_index(axis) & bit) != 0
    both = jnp.stack([value, value], axis=spot)
    return lax.dynamic_update_index_in_dim(both, other, jnp.where(up, 0, 1), spot)


def gather_rows(rows, pair=False):
    gx, g = lax.axis_size("gx"), lax.axis_size("gy") // lax.axis_size("gx")
    if pair:
        rows = joined(rows, 1, 0, "gx").reshape(-1, rows.shape[1])
    n, width = rows.shape
    if lax.axis_size("gy") != 8:
        whole = lax.all_gather(rows, "gy", axis=0, tiled=True).reshape(gx, g, n, width)
        return jnp.swapaxes(whole, 0, 1).reshape(-1, width)
    half = width // 2
    left, right = rows[:, :half], rows[:, half:]
    left = joined(joined(left, 2, 0), 4, 0)
    right = joined(joined(right, 4, 0), 2, 1)
    both = [joined(v.reshape(4 * n, half), 1, 0).reshape(8 * n, half) for v in (left, right)]
    return jnp.concatenate(both, axis=1)


def reduced(value, bit, spot, axis="gy"):
    up = jnp.where((lax.axis_index(axis) & bit) != 0, 1, 0)
    send = lax.dynamic_index_in_dim(value, 1 - up, spot, keepdims=False).astype(BF16)
    keep = lax.dynamic_index_in_dim(value, up, spot, keepdims=False)
    return keep + swap(send, bit, axis).astype(F32)


def project_sum(left, weight, dims, pair=False):
    return summed_projection(left, weight, dims, pair)


def summed_projection(left, weight, dims, pair):
    gx, g = lax.axis_size("gx"), lax.axis_size("gy") // lax.axis_size("gx")
    n = left.shape[0] // (gx * g)
    if lax.axis_size("gy") != 8:
        left = jnp.swapaxes(left.reshape(g, gx, n, -1), 0, 1).reshape(left.shape)
        part = dot(left, weight, dims).astype(BF16)
        total = lax.psum_scatter(part, "gy", scatter_dimension=0, tiled=True).astype(F32)
    else:
        up = lax.axis_index("gy") & 1
        left = left.reshape(2, 4 * n, -1)
        other = swap(dot(at(left, 1 - up), weight, dims).astype(BF16), 1)
        total = dot(at(left, up), weight, dims) + other.astype(F32)
        total = total.reshape(2, 2, n, -1)
        half = total.shape[3] // 2
        left_half = reduced(reduced(total[..., :half], 4, 0), 2, 0)
        right_half = reduced(reduced(total[..., half:], 2, 1), 4, 0)
        total = jnp.concatenate([left_half, right_half], axis=1)
    if pair:
        total = reduced(total.reshape(2, n // 2, -1), 1, 0, "gx")
    return total


def whole_width(local):
    gx = lax.axis_size("gx")
    i = lax.axis_index("gx")
    came = [local] + [
        lax.ppermute(local, "gx", [(a, (a + k) % gx) for a in range(gx)]) for k in range(1, gx)
    ]
    return jnp.concatenate([lax.select_n((i - a) % gx, *came) for a in range(gx)], axis=-1)


def sum_width(parts):
    gx, gy = lax.axis_size("gx"), lax.axis_size("gy")
    i = lax.axis_index("gx")
    width = parts.shape[-1] // gx
    blocks = [parts[..., a * width : (a + 1) * width] for a in range(gx)]
    total = lax.select_n(i, *blocks)
    for k in range(1, gx):
        send = lax.select_n((i + k) % gx, *blocks)
        total = total + lax.ppermute(send, "gx", [(a, (a + k) % gx) for a in range(gx)])
    bit = 1
    while bit < gy:
        total = total + swap(total, bit)
        bit *= 2
    return total


def after(value, *first):
    return lax.optimization_barrier((value,) + first)[0]


def normalize(value, gain):
    scale = lax.rsqrt(jnp.mean(value * value, axis=1, keepdims=True) + EPS)
    return (value * scale * gain[None, :]).astype(BF16), scale


def normalize_back(value, gain, scale, grad):
    weighted = grad * gain[None, :]
    inner = jnp.mean(weighted * value, axis=1, keepdims=True)
    grad_gain = jnp.sum(grad * value * scale, axis=0)
    return scale * weighted - value * (scale * scale * scale * inner), grad_gain


def doc_starts(segs):
    index = jnp.broadcast_to(jnp.arange(segs.shape[1], dtype=jnp.int32)[None, :], segs.shape)
    before = jnp.concatenate([segs[:, :1] - 1, segs[:, :-1]], axis=1)
    return lax.cummax(jnp.where(segs != before, index, jnp.zeros_like(index)), axis=1)


def rotary(positions, width):
    half = HD // 2
    freq = THETA ** (-jnp.arange(half, dtype=F32) * 2.0 / HD)
    angle = positions.astype(F32)[:, None] * freq[None, :]
    copies = width // half
    return jnp.tile(jnp.cos(angle), (1, copies)), jnp.tile(jnp.sin(angle), (1, copies))


def turn(value):
    width = value.shape[1]
    half = HD // 2
    pieces = []
    for at in range(0, width, HD):
        pieces += [-value[:, at + half : at + HD], value[:, at : at + half]]
    return jnp.concatenate(pieces, axis=1)


def masked_scores(query, key, start, first):
    scores = dot(query, key, ((1,), (1,)))
    kidx = lax.broadcasted_iota(jnp.int32, scores.shape, 1)
    qidx = lax.broadcasted_iota(jnp.int32, scores.shape, 0) + first
    return jnp.where((kidx >= start) & (kidx <= qidx), scores, NEG)


def forward_kernel(block, q_ref, k_ref, v_ref, cos_ref, sin_ref, start_ref, att, qo, ko, vo, lse):
    cosine, sine = cos_ref[...], sin_ref[...]
    q, k = q_ref[...], k_ref[...]
    qo[...] = (q * cosine + turn(q) * sine).astype(BF16)
    ko[...] = (k * cosine + turn(k) * sine).astype(BF16)
    vo[...] = v_ref[...].astype(BF16)
    length, width = q.shape
    for at in range(0, width, HD):
        lanes = slice(at, at + HD)
        for first in range(0, length, block):
            rows, high = slice(first, first + block), first + block
            query = qo[rows, lanes] * BF16(HD**-0.5)
            scores = masked_scores(query, ko[:high, lanes], start_ref[rows, :], first)
            peak = jnp.max(scores, axis=1, keepdims=True)
            expo = jnp.exp(scores - peak)
            total = jnp.sum(expo, axis=1, keepdims=True)
            probs = (expo / total).astype(BF16)
            att[rows, lanes] = dot(probs, vo[:high, lanes], ((1,), (0,))).astype(BF16)
            lse[rows, lanes] = jnp.broadcast_to(peak + jnp.log(total), (block, HD))


def backward_kernel(block, q, k, v, g, lse, cos_ref, sin_ref, start_ref, dqo, dko, dvo, dq, dk, dv):
    length, width = q.shape
    dk[...] = jnp.zeros_like(dk)
    dv[...] = jnp.zeros_like(dv)
    for at in range(0, width, HD):
        lanes = slice(at, at + HD)
        for first in range(0, length, block):
            rows, high = slice(first, first + block), first + block
            query = q[rows, lanes] * BF16(HD**-0.5)
            key, grad = k[:high, lanes], g[rows, lanes]
            scores = masked_scores(query, key, start_ref[rows, :], first)
            probs = jnp.exp(scores - lse[rows, at : at + 1])
            dprob = dot(grad, v[:high, lanes], ((1,), (1,)))
            delta = jnp.sum(probs * dprob, axis=1, keepdims=True)
            draw = (probs * (dprob - delta)).astype(BF16)
            dq[rows, lanes] = dot(draw, key, ((1,), (0,))) * HD**-0.5
            dk[:high, lanes] += dot(draw, query, ((0,), (0,)))
            dv[:high, lanes] += dot(probs.astype(BF16), grad, ((0,), (0,)))
    cosine, sine = cos_ref[...], sin_ref[...]
    dqo[...] = (dq[...] * cosine - turn(dq[...] * sine)).astype(BF16)
    dko[...] = (dk[...] * cosine - turn(dk[...] * sine)).astype(BF16)
    dvo[...] = dv[...].astype(BF16)


def attention_specs(seqs, length, wide):
    lanes = min(128, wide)
    pairs = wide // lanes
    grid = (seqs, pairs)
    own = pl.BlockSpec((length, lanes), lambda s, p: (s, p))
    table = pl.BlockSpec((length, lanes), lambda s, p: (s, 0))
    starts = pl.BlockSpec((length, 1), lambda s, p: (s, 0))
    return grid, lanes, pairs, own, table, starts


def attend_forward(pre, cosine, sine, starts, seqs):
    rows, wide = pre.shape[0], pre.shape[1] // 3
    length = rows // seqs
    grid, lanes, pairs, own, table, start_spec = attention_specs(seqs, length, wide)
    if lanes == 128:
        parts = (pre, pre, pre)
        specs = [
            pl.BlockSpec((length, lanes), functools.partial(lambda c, s, p: (s, c * pairs + p), c))
            for c in range(3)
        ]
    else:
        parts = tuple(pre[:, c * wide : (c + 1) * wide] for c in range(3))
        specs = [own] * 3
    low = jax.ShapeDtypeStruct((rows, wide), BF16)
    return pl.pallas_call(
        functools.partial(forward_kernel, min(256, length)),
        grid=grid,
        in_specs=specs + [table, table, start_spec],
        out_specs=[own] * 5,
        out_shape=[low] * 4 + [jax.ShapeDtypeStruct((rows, wide), F32)],
        name="attend_forward",
    )(*parts, cosine, sine, starts)


def attend_backward(query, key, value, grad, lse, cosine, sine, starts, seqs):
    rows, wide = query.shape
    length = rows // seqs
    grid, lanes, _, own, table, start_spec = attention_specs(seqs, length, wide)
    low = jax.ShapeDtypeStruct((rows, wide), BF16)
    return pl.pallas_call(
        functools.partial(backward_kernel, min(256, length)),
        grid=grid,
        in_specs=[own] * 5 + [table, table, start_spec],
        out_specs=[own] * 3,
        out_shape=[low] * 3,
        scratch_shapes=[pltpu.VMEM((length, lanes), F32)] * 3,
        name="attend_backward",
    )(query, key, value, grad, lse, cosine, sine, starts)


def gather_in(weight):
    return lax.all_gather(weight, "gx", axis=0, tiled=True)


def gather_out(weight):
    whole = lax.all_gather(weight, "gx", axis=0)
    return jnp.swapaxes(whole, 0, 1).reshape(weight.shape[0], -1)


def sum_in(part):
    return lax.psum_scatter(part, "gx", scatter_dimension=0, tiled=True).astype(F32)


def grad_out_of(cols, grad):
    gx = lax.axis_size("gx")
    width = grad.shape[1] // gx
    parts = [
        dot(cols, grad[:, a * width : (a + 1) * width], ((0,), (0,))).astype(BF16)
        for a in range(gx)
    ]
    return jnp.stack(parts)


def sum_out(part):
    return lax.psum_scatter(part, "gx", scatter_dimension=0, tiled=False).astype(F32)


def far_planes():
    gx = lax.axis_size("gx")
    return [list(range(parity, gx, 2)) for parity in range(2)]


def own_and_other(low, high):
    odd = lax.axis_index("gx") & 1
    return pick([low, high], odd), pick([high, low], odd)


def halves_from_planes(low, high):
    own, other = own_and_other(low, high)
    near = joined_with(own, swap(other, 1, "gx"), 1, 0, "gx")
    return lax.all_gather(near, "gx", axis=0, tiled=True, axis_index_groups=far_planes())


def sum_of_halves(part):
    return lax.psum_scatter(
        part, "gx", scatter_dimension=0, tiled=True, axis_index_groups=far_planes()
    )


def halves_to_planes(near):
    odd = lax.axis_index("gx") & 1
    own = at(near, odd)
    other = swap(at(near, 1 - odd), 1, "gx")
    return own_and_other(own.astype(F32), other.astype(F32))


IN = ((1,), (0,))
BACK = ((1,), (1,))
TOKENS = ((0,), (0,))


def layer(tokens, gain_attn, w_qkv, w_out, gain_mlp, w_gate_up, w_down, segments, grad_output):
    gx = lax.axis_size("gx")
    seqs, length = segments.shape
    wide = w_qkv.shape[2]
    width = w_down.shape[0] // 2

    wq = gather_in(w_qkv.reshape(w_qkv.shape[0], -1))
    wo = gather_out(w_out)

    low_x = to_rows(tokens)
    x = low_x.astype(F32)
    small, dy_in = after((jnp.stack([gain_attn, gain_mlp]), grad_output), low_x)
    gains = whole_width(small)
    normed_a, scale_a = normalize(x, gains[0])
    rows_a = gather_rows(normed_a)

    gu = [
        jnp.concatenate([w_gate_up[:, 0, h : h + width], w_gate_up[:, 1, h : h + width]], axis=1)
        for h in (0, width)
    ]
    dy_in, gu, down = after((dy_in, gu, [w_down[:width], w_down[width:]]), normed_a)
    wgu = halves_from_planes(*gu).reshape(-1, 2 * width)
    wd = halves_from_planes(*down)
    wd = jnp.swapaxes(wd.reshape(-1, width, w_down.shape[1]), 0, 1).reshape(width, -1)
    dy_low = to_rows(dy_in)
    dy_rows = gather_rows(dy_low, True)

    starts = doc_starts(segments)
    positions = jnp.arange(length, dtype=jnp.int32)[None, :] - starts
    cosine, sine = rotary(positions.reshape(-1), min(128, wide))
    starts = starts.reshape(-1, 1)

    rows_a = after(rows_a, cosine, sine)
    pre = dot(rows_a, wq, IN)
    att, query, key, value, lse = attend_forward(pre, cosine, sine, starts, seqs)
    mid = x + project_sum(att, wo, IN)

    normed_m, scale_m = normalize(mid, gains[1])
    rows_m = gather_rows(normed_m, True)
    gate_up = dot(rows_m, wgu, IN)
    gate, up = gate_up[:, :width], gate_up[:, width:]
    sig = jax.nn.sigmoid(gate)
    hidden = (gate * sig * up).astype(BF16)
    down_part = grad_out_of(hidden, dy_rows)
    down_sum = sum_of_halves(down_part)
    dhid = dot(after(dy_rows, down_part), wd, BACK)
    dgate = dhid * up * sig * (1.0 + gate * (1.0 - sig))
    dup = dhid * gate * sig
    dgu = jnp.concatenate([dgate, dup], axis=1).astype(BF16)
    gate_up_part = dot(rows_m, dgu, TOKENS).astype(BF16)
    gate_up_sum = sum_of_halves(gate_up_part.reshape(gx, -1, 2 * width))
    dnormed_m = project_sum(after(dgu, gate_up_part), wgu, BACK, True)

    dmid_norm, gain_m = normalize_back(mid, gains[1], scale_m, dnormed_m)
    dmid = dy_low.astype(F32) + dmid_norm
    dmid_rows = gather_rows(dmid.astype(BF16))
    out_part = grad_out_of(att, dmid_rows)
    datt = dot(after(dmid_rows, out_part), wo, BACK).astype(BF16)
    dpre = attend_backward(query, key, value, datt, lse, cosine, sine, starts, seqs)
    dpre = jnp.concatenate(dpre, axis=1)
    qkv_part = dot(rows_a, dpre, TOKENS).astype(BF16)
    dnormed_a = project_sum(after(dpre, qkv_part), wq, BACK)
    dx_norm, gain_a = normalize_back(x, gains[0], scale_a, dnormed_a)
    grad_tokens = to_blocks((dmid + dx_norm).astype(BF16)).astype(F32)
    output = mid + project_sum(after(hidden, datt), wd, IN, True)

    down_low, down_high = halves_to_planes(down_sum)
    gu_low, gu_high = halves_to_planes(gate_up_sum)
    grad_gate_up = jnp.stack(
        [
            jnp.concatenate([gu_low[:, at : at + width], gu_high[:, at : at + width]], axis=1)
            for at in (0, width)
        ],
        axis=1,
    )
    return (
        to_blocks(output.astype(BF16)),
        grad_tokens,
        sum_width(gain_a),
        sum_in(qkv_part).reshape(w_qkv.shape),
        sum_out(out_part),
        sum_width(gain_m),
        grad_gate_up,
        jnp.concatenate([down_low, down_high], axis=0),
    )


def solution(mesh):
    in_specs = (
        P("gy", "gx"),
        P("gx"),
        P("gx", None, "gy"),
        P("gy", "gx"),
        P("gx"),
        P("gx", None, "gy"),
        P("gy", "gx"),
        P("gx", None),
        P("gy", "gx"),
    )
    out_specs = (
        P("gy", "gx"),
        P("gy", "gx"),
        P("gx"),
        P("gx", None, "gy"),
        P("gy", "gx"),
        P("gx"),
        P("gx", None, "gy"),
        P("gy", "gx"),
    )
    return jax.shard_map(layer, mesh=mesh, in_specs=in_specs, out_specs=out_specs, check_vma=False)
```
